1024 devices in a mesh: inner: 16 (over z_lo, core), outer: 64 (over x, y, z_hi).
Axes of the slice: x: 4, y: 8, z: 16 (z_hi: 2, z_lo: 8; z = z_hi * 8 + z_lo), core: 2. Of those that a mesh axis runs over, the one named last changes fastest.
Arguments:
- tokens: bfloat16 [131072, 4096], P(('inner', 'outer')), may hold values from -24 to 24
- weight_codes: bfloat16 [4096, 512], P('inner'), may hold values from -127 to 127
- scales: float32 [1024], P('inner'), may hold values from 0.00012 to 0.0004
- cotangent: bfloat16 [131072, 512], P(('inner', 'outer')), may hold values from -6 to 6
Outputs:
- keys: bfloat16 [131072, 512], P(('inner', 'outer'))
- grad_tokens: bfloat16 [131072, 4096], P(('inner', 'outer'))
- grad_weight: float32 [4096, 512], P(('inner', 'outer'))
The draws below stay inside these ranges and needn't reach their ends.
All inputs are finite; a program needn't handle non-finite values.
Results may differ from the reference program's by a relative error of at most 0.017.
Values may be sent and summed in bfloat16 or wider, within the bound.
A program may use at most 64 MiB of HBM per device.

```python
import math
import jax
import jax.numpy as jnp
from jax import lax

D = 4096
TOK_DEV = 128
KV = 512
QROWS = 4
TOKENS = 131072
N_INNER = 16
N_OUTER = 64


def spiked(values, rng, source, target, parts, factor):
    def block_of(dim):
        return (jnp.arange(values.shape[dim]) // (values.shape[dim] // parts)).reshape((-1,) + (1,) * (values.ndim - 1 - dim))

    first = jax.random.permutation(rng, parts)[block_of(target)]
    second = (block_of(target) + parts // 2) % parts
    return jnp.where((block_of(source) == first) | (block_of(source) == second), factor * values, values)


def block_scale(rng, dims, split, low, largest):
    factor_of, own = 1.0, jax.random.fold_in(rng, 6)
    for position, blocks in split:
        steps = jnp.exp(jax.random.uniform(jax.random.fold_in(own, position), (blocks,), jnp.float32, low / len(split), largest / len(split)))
        factor_of = factor_of * jnp.repeat(steps, dims[position] // blocks).reshape([-1 if axis == position else 1 for axis in range(len(dims))])
    return factor_of


def centred(own_key, shape, spread, most, shards=(), kind=jnp.bfloat16):
    result = spread * jax.random.normal(own_key, shape, jnp.float32)
    if shards:
        result = result * block_scale(own_key, shape, shards, -0.22, 0.18)
    return jnp.clip(result, -most, most).astype(kind)


def bell_draw_with(rng, extent, scale, bound, shards, heavy, dtype=jnp.bfloat16):
    array = scale * jax.random.normal(rng, extent, jnp.float32)
    if shards:
        array = array * block_scale(rng, extent, shards, -0.22, 0.18)
    return jnp.clip(spiked(array, jax.random.fold_in(rng, 3), *heavy), -bound, bound).astype(dtype)


def setup_inputs(seed: int = 0) -> dict:
    key_of = jax.random.split(jax.random.key(seed), 5)
    tokens = bell_draw_with(key_of[0], (TOKENS, D), 1.0, 24.0, ((0, 1024),), (0, 1, 1024, 6.0))
    weight_codes = jnp.clip(jax.random.uniform(key_of[1], (D, KV), jnp.float32, -127.0, 127.0) * block_scale(key_of[1], (D, KV), ((0, 16),), -0.4, 0.0), -127.0, 127.0).astype(jnp.bfloat16)
    scales = jnp.clip(jnp.exp(math.log(0.0004) - 1.2039728 * jax.random.uniform(key_of[2], (D // QROWS,), jnp.float32) ** block_scale(key_of[2], (D // QROWS,), ((0, 16),), -0.2, 0.2)), 0.00012, 0.0004)
    cotangent = centred(key_of[3], (TOKENS, KV), 1.0, 6.0, ((0, 1024),))
    return dict(tokens=tokens, weight_codes=weight_codes, scales=scales, cotangent=cotangent)


EPS = 1e-05

def block_pass(block_x, block_ct, weight):
    xf = block_x.astype(jnp.float32)
    inv_norm = lax.rsqrt(lax.optimization_barrier(jnp.mean(xf * xf, axis=-1, keepdims=True)) + EPS)
    normed_f = xf * inv_norm
    normed = normed_f.astype(jnp.bfloat16)
    keys = jnp.dot(normed, weight, preferred_element_type=jnp.float32).astype(jnp.bfloat16)
    grad_normed = lax.dot_general(block_ct, weight, (((1,), (1,)), ((), ())), preferred_element_type=jnp.float32)
    inner_mean = lax.optimization_barrier(jnp.mean(grad_normed * normed_f, axis=-1, keepdims=True))
    grad_x = (inv_norm * (grad_normed - normed_f * inner_mean)).astype(jnp.bfloat16)
    partial_value = lax.dot_general(normed, block_ct, (((0,), (0,)), ((), ())), preferred_element_type=jnp.float32)
    partial_value = lax.optimization_barrier(partial_value.astype(jnp.bfloat16)).astype(jnp.float32)
    return (keys, grad_x, partial_value)

def reference(tokens, weight_codes, scales, cotangent):
    devices_all = N_INNER * N_OUTER
    scaled = weight_codes.astype(jnp.float32).reshape(D // QROWS, QROWS * KV) * scales[:, None]
    weight = scaled.reshape(D, KV).astype(jnp.bfloat16)
    blocks_x = tokens.reshape(devices_all, TOK_DEV, D)
    blocks_ct = cotangent.reshape(devices_all, TOK_DEV, KV)

    def stepper(total, pair):
        keys, grad_x, partial_value = block_pass(pair[0], pair[1], weight)
        return (total + partial_value, (keys, grad_x))
    start_total = jnp.zeros((D, KV), jnp.float32)
    grad_weight, outs = lax.scan(stepper, start_total, (blocks_x, blocks_ct))
    keys = outs[0].reshape(TOKENS, KV)
    grad_tokens = outs[1].reshape(TOKENS, D)
    return (keys, grad_tokens, grad_weight)
```

```python
import jax
import jax.numpy as jnp
from jax import lax
from jax.experimental import pallas as pl
from jax.experimental.pallas import tpu as pltpu
from jax.sharding import PartitionSpec as P

EPS = 1e-05
NX, NY, NZL, NZ = 4, 8, 8, 16
TOK, D, KV = 128, 4096, 512
ROWS = 256
HALF = ROWS // 2
LANE = 128
N_SEM = 96
MESH = pl.DeviceIdType.MESH
F32, BF16 = jnp.float32, jnp.bfloat16


def kernel(
    tok, codes, scales, cot, keys, grad_tokens, grad_weight,
    inv, nb, pair_n, pair_c, part, wbuf, gn, gt, kacc, macc,
    ys, yr, xs, xr, ra, rb, xds, xdr, yds, ydr, fin, zf, zs, zr,
    send_sem, recv_sem, out_sem, near, far,
):
    inner, outer = lax.axis_index("inner"), lax.axis_index("outer")
    c, zl = lax.rem(inner, 2), lax.div(inner, 2)
    zh, y, x = lax.rem(outer, 2), lax.rem(lax.div(outer, 2), NY), lax.div(outer, 2 * NY)
    z = zh * NZL + zl

    def at(nx, ny, nz, nc):
        return (lax.rem(nz, NZL) * 2 + nc, (nx * NY + ny) * 2 + lax.div(nz, NZL))

    def x_off(d):
        return lax.rem(x + d + NX, NX)

    def y_off(d):
        return lax.rem(y + d + NY, NY)

    def z_off(d):
        return lax.rem(z + d + NZ, NZ)

    def on_x(d):
        return at(x_off(d), y, z, c)

    def on_y(d):
        return at(x, y_off(d), z, c)

    def on_z(d):
        return at(x, y, z_off(d), c)

    partner = at(x, y, z, 1 - c)
    copies = []

    def send(src, dst, device):
        n = len(copies)
        copy = pltpu.make_async_remote_copy(
            src_ref=src, dst_ref=dst, send_sem=send_sem.at[n], recv_sem=recv_sem.at[n],
            device_id=device, device_id_type=MESH,
        )
        copy.start()
        copies.append(copy)
        return copy

    barrier = pltpu.get_barrier_semaphore()
    for device in (partner, on_z(1), on_z(-1), on_y(1), on_y(-1), on_x(1), on_x(-1)):
        pl.semaphore_signal(barrier, inc=1, device_id=device, device_id_type=MESH)

    groups = scales.shape[1]
    row = lax.broadcasted_iota(jnp.int32, (ROWS, groups), 0)
    col = lax.broadcasted_iota(jnp.int32, (ROWS, groups), 1)
    per_row = jnp.where(lax.div(row, ROWS // groups) == col, scales[...], 0.0)
    per_row = jnp.sum(per_row, axis=1, keepdims=True)
    wbuf[0, c] = (codes[...].astype(F32) * per_row).astype(BF16)

    pl.semaphore_wait(barrier, 7)

    got = {}

    def slot_of(way, k):
        return k if way > 0 or k in (0, 4) else 4 + k

    def rows_of(h):
        return pl.ds(h * HALF, HALF)

    def pass_on(way, k, h):
        got[way, k + 1, h] = send(
            wbuf.at[slot_of(way, k), c, rows_of(h)],
            wbuf.at[slot_of(way, k + 1), c, rows_of(h)],
            on_z(way),
        )

    def relay(slot, h):
        got["relay", slot, h] = send(
            wbuf.at[slot, c, rows_of(h)], wbuf.at[slot, c, rows_of(h)], partner
        )

    def arrive(way, k, h):
        got[way, k, h].wait_recv()
        if k < 3 or (k == 3 and h == (0 if way > 0 else 1)):
            pass_on(way, k, h)
        relay(slot_of(way, k), h)

    pass_on(1, 0, 0)
    pass_on(-1, 0, 1)
    pass_on(1, 0, 1)
    pass_on(-1, 0, 0)
    relay(0, 0)
    relay(0, 1)
    for d in (1, -1):
        pl.semaphore_signal(near.at[0], inc=1, device_id=on_y(d), device_id_type=MESH)

    total = jnp.zeros((TOK, LANE), F32)
    for k in range(D // LANE):
        v = tok[:, k * LANE : (k + 1) * LANE].astype(F32)
        total = total + v * v
    mean = jnp.sum(total, axis=1, keepdims=True) * (1.0 / D)
    inv[...] = jnp.broadcast_to(lax.rsqrt(mean + EPS), (TOK, LANE))
    for k in range(D // LANE):
        v = (tok[:, k * LANE : (k + 1) * LANE].astype(F32) * inv[...]).astype(BF16)
        strip = k // 2
        nb[strip % 2, strip // 2, :, (k % 2) * LANE : (k % 2 + 1) * LANE] = v

    n_copy = send(nb.at[1 - c], pair_n.at[:, pl.ds(TOK, TOK)], partner)
    c_copy = send(cot, pair_c.at[pl.ds(TOK, TOK)], partner)
    pair_c[:TOK] = cot[...]
    pair_n[:, :TOK] = nb[c]
    pl.semaphore_wait(near.at[0], 2)
    for d in (2, -2):
        pl.semaphore_signal(near.at[1], inc=1, device_id=on_y(d), device_id_type=MESH)
    c_copy.wait_recv()
    n_copy.wait_recv()

    def part_rows(b, _):
        p = lax.dot_general(
            pair_n[b], pair_c[...], (((0,), (0,)), ((), ())), preferred_element_type=F32
        )
        part[b] = p.reshape(NX, NY, 8, KV)
        return _

    lax.fori_loop(0, NZL, part_rows, 0)

    def lanes(color, j):
        return slice((color * 2 + j) * LANE, (color * 2 + j + 1) * LANE)

    def y_part(d, j):
        return part[:, :, y_off(d), :, lanes(0, j)].reshape(NZL * NX * 8, LANE)

    def x_part(d, j):
        return part[:, x_off(d), :, :, lanes(1, j)].reshape(NZL * NY * 8, LANE)

    ring = {}

    def hop(axis, way, j, s):
        n, mine, out, into, on = (
            (NY, y_part, ys, yr, on_y) if axis == "y" else (NX, x_part, xs, xr, on_x)
        )
        last = n // 2
        w = 0 if way > 0 else 1
        first = 1 if j == w else 2
        v = mine(way * (last + 1 - s), j)
        if s > first:
            ring[axis, way, j, s - 1].wait_recv()
            v = v + into[w, j, s - 2].astype(F32)
        out[w, j, s - 1] = v.astype(BF16)
        ring[axis, way, j, s] = send(out.at[w, j, s - 1], into.at[w, j, s - 1], on(way))

    def ring_sum(axis, j):
        n, mine, into = (NY, y_part, yr) if axis == "y" else (NX, x_part, xr)
        v = mine(0, j)
        for w, way in enumerate((1, -1)):
            ring[axis, way, j, n // 2].wait_recv()
            v = v + into[w, j, n // 2 - 1].astype(F32)
        return v

    def y_ring_end():
        for j in range(2):
            ra[:, :, :, j * LANE : (j + 1) * LANE] = ring_sum("y", j).reshape(NZL, NX, 8, LANE)

    def x_ring_end():
        for j in range(2):
            rb[:, :, :, j * LANE : (j + 1) * LANE] = ring_sum("x", j).reshape(NZL, NY, 8, LANE)

    direct = {}

    def x_direct():
        for d in range(1, NX):
            xds[d - 1] = ra[:, x_off(d)].reshape(NZL * 8, 2 * LANE).astype(BF16)
            direct["x", d] = send(xds.at[d - 1], xdr.at[d - 1], on_x(d))

    def x_direct_end():
        v = ra[:, x].reshape(NZL * 8, 2 * LANE)
        for d in range(1, NX):
            direct["x", d].wait_recv()
            v = v + xdr[d - 1].astype(F32)
        fin[:, :, : 2 * LANE] = v.reshape(NZL, 8, 2 * LANE)

    def y_direct():
        pl.semaphore_wait(near.at[1], 2)
        for d in range(1, NY):
            yds[d - 1] = rb[:, y_off(d)].reshape(NZL * 8, 2 * LANE).astype(BF16)
            direct["y", d] = send(yds.at[d - 1], ydr.at[d - 1], on_y(d))

    def y_direct_end():
        v = rb[:, y].reshape(NZL * 8, 2 * LANE)
        for d in range(1, NY):
            direct["y", d].wait_recv()
            v = v + ydr[d - 1].astype(F32)
        fin[:, :, 2 * LANE :] = v.reshape(NZL, 8, 2 * LANE)

    def z_direct():
        for h in range(2):
            v = jnp.concatenate(
                [fin[:, h * 4 : h * 4 + 4, k * LANE : (k + 1) * LANE] for k in range(4)], axis=1
            )
            zf[h] = v
            zs[h] = v.astype(BF16)
        pl.semaphore_wait(far.at[0], 1)
        pl.semaphore_wait(far.at[1], 1)
        for d in range(1, NZ):
            to = z_off(d)
            direct["z", d] = send(
                zs.at[lax.div(to, NZL), lax.rem(to, NZL)], zr.at[d - 1], on_z(d)
            )

    def z_direct_end():
        v = zf[zh, zl]
        for d in range(1, NZ):
            direct["z", d].wait_recv()
            v = v + zr[d - 1].astype(F32)
        for k in range(4):
            grad_weight[:, k * LANE : (k + 1) * LANE] = v[k * 4 : k * 4 + 4]

    kacc[...] = jnp.zeros_like(kacc)
    macc[...] = jnp.zeros_like(macc)

    def chip_of(slot):
        return lax.rem(zl + (NZL - slot if slot < 4 else slot if slot == 4 else slot - 4), NZL)

    def use(slot):
        b = chip_of(slot)
        for h in range(2):
            got["relay", slot, h].wait_recv()
        for p in range(2):
            w = wbuf[slot, p]
            kacc[...] += jnp.dot(nb[p, b], w, preferred_element_type=F32)
            g = lax.dot_general(
                cot[...], w, (((1,), (1,)), ((), ())), preferred_element_type=F32
            )
            gn[b, :, p * ROWS : (p + 1) * ROWS] = g
            for q in range(2):
                off = pl.multiple_of(b * (2 * ROWS) + (p * 2 + q) * LANE, LANE)
                nf = tok[:, pl.ds(off, LANE)].astype(F32) * inv[...]
                macc[...] += g[:, q * LANE : (q + 1) * LANE] * nf

    out_copies = []

    def finish_tokens():
        keys[...] = kacc[...].astype(BF16)
        inner_mean = jnp.sum(macc[...], axis=1, keepdims=True) * (1.0 / D)
        macc[...] = jnp.broadcast_to(inner_mean, (TOK, LANE))

        def strip(b, _):
            for q in range(4):
                off = pl.multiple_of(b * (4 * LANE) + q * LANE, LANE)
                nf = tok[:, pl.ds(off, LANE)].astype(F32) * inv[...]
                g = gn[b, :, q * LANE : (q + 1) * LANE]
                gt[:, pl.ds(off, LANE)] = (inv[...] * (g - nf * macc[...])).astype(BF16)
            return _

        lax.fori_loop(0, NZL, strip, 0)
        copy = pltpu.make_async_copy(gt, grad_tokens, out_sem)
        copy.start()
        out_copies.append(copy)

    def both(f, *args):
        k, first = args
        f(1, k, 0 if first else 1)
        f(-1, k, 1 if first else 0)

    def hops(axis, s, first):
        hop(axis, 1, 0 if first else 1, s)
        hop(axis, -1, 1 if first else 0, s)

    def far_signals():
        pl.semaphore_signal(far.at[0], inc=1, device_id=on_z(4), device_id_type=MESH)
        pl.semaphore_signal(far.at[1], inc=1, device_id=on_z(-4), device_id_type=MESH)

    hops("y", 1, True)
    hops("x", 1, True)
    hops("y", 2, False)
    hops("x", 2, False)
    both(arrive, 1, True)
    use(0)
    both(arrive, 1, False)
    hops("y", 2, True)
    both(arrive, 2, True)
    hops("y", 3, False)
    hops("x", 2, True)
    use(1)
    both(arrive, 2, False)
    hops("y", 3, True)
    hops("y", 4, False)
    use(5)
    both(arrive, 3, True)
    x_ring_end()
    y_direct()
    hops("y", 4, True)
    both(arrive, 3, False)
    use(2)
    use(6)
    y_ring_end()
    x_direct()
    both(arrive, 4, True)
    far_signals()
    use(3)
    use(7)
    use(4)
    x_direct_end()
    y_direct_end()
    z_direct()
    finish_tokens()
    z_direct_end()
    for copy in copies:
        copy.wait_send()
    for copy in out_copies:
        copy.wait()


def local(tokens, weight_codes, scales, cotangent):
    vmem = pl.BlockSpec(memory_space=pltpu.VMEM)
    return pl.pallas_call(
        kernel,
        out_shape=(
            jax.ShapeDtypeStruct((TOK, KV), BF16),
            jax.ShapeDtypeStruct((TOK, D), BF16),
            jax.ShapeDtypeStruct((4, KV), F32),
        ),
        in_specs=[vmem] * 4,
        out_specs=(vmem, pl.BlockSpec(memory_space=pl.ANY), vmem),
        scratch_shapes=[
            pltpu.VMEM((TOK, LANE), F32),
            pltpu.VMEM((2, NZL, TOK, ROWS), BF16),
            pltpu.VMEM((NZL, 2 * TOK, ROWS), BF16),
            pltpu.VMEM((2 * TOK, KV), BF16),
            pltpu.VMEM((NZL, NX, NY, 8, KV), F32),
            pltpu.VMEM((8, 2, ROWS, KV), BF16),
            pltpu.VMEM((NZL, TOK, 2 * ROWS), F32),
            pltpu.VMEM((TOK, D), BF16),
            pltpu.VMEM((TOK, KV), F32),
            pltpu.VMEM((TOK, LANE), F32),
            pltpu.VMEM((2, 2, NY // 2, NZL * NX * 8, LANE), BF16),
            pltpu.VMEM((2, 2, NY // 2, NZL * NX * 8, LANE), BF16),
            pltpu.VMEM((2, 2, NX // 2, NZL * NY * 8, LANE), BF16),
            pltpu.VMEM((2, 2, NX // 2, NZL * NY * 8, LANE), BF16),
            pltpu.VMEM((NZL, NX, 8, 2 * LANE), F32),
            pltpu.VMEM((NZL, NY, 8, 2 * LANE), F32),
            pltpu.VMEM((NX - 1, NZL * 8, 2 * LANE), BF16),
            pltpu.VMEM((NX - 1, NZL * 8, 2 * LANE), BF16),
            pltpu.VMEM((NY - 1, NZL * 8, 2 * LANE), BF16),
            pltpu.VMEM((NY - 1, NZL * 8, 2 * LANE), BF16),
            pltpu.VMEM((NZL, 8, KV), F32),
            pltpu.VMEM((2, NZL, 16, LANE), F32),
            pltpu.VMEM((2, NZL, 16, LANE), BF16),
            pltpu.VMEM((NZ - 1, 16, LANE), BF16),
            pltpu.SemaphoreType.DMA((N_SEM,)),
            pltpu.SemaphoreType.DMA((N_SEM,)),
            pltpu.SemaphoreType.DMA,
            pltpu.SemaphoreType.REGULAR((2,)),
            pltpu.SemaphoreType.REGULAR((2,)),
        ],
        compiler_params=pltpu.CompilerParams(collective_id=0, has_side_effects=True),
        name="key_projection",
    )(tokens, weight_codes, scales.reshape(1, -1), cotangent)


def solution(mesh):
    in_specs = (
        P(("inner", "outer"), None),
        P("inner", None),
        P("inner"),
        P(("inner", "outer"), None),
    )
    out_specs = (P(("inner", "outer"), None),) * 3
    return jax.shard_map(local, mesh=mesh, in_specs=in_specs, out_specs=out_specs, check_vma=False)
```

```python
import jax
import jax.numpy as jnp
from jax import lax
from jax.experimental import pallas as pl
from jax.experimental.pallas import tpu as pltpu
from jax.sharding import PartitionSpec as P

EPS = 1e-05
NX, NY, NZL, NZ = 4, 8, 8, 16
TOK, D, KV = 128, 4096, 512
ROWS = 256
HALF = ROWS // 2
LANE = 128
N_SEM = 112
OUT = pltpu.VMEM
MESH = pl.DeviceIdType.MESH
F32, BF16 = jnp.float32, jnp.bfloat16


def kernel(
    tok_h, codes_h, scales_h, cot_h, keys, grad_tokens, grad_weight,
    tok, codes, scales, cot, inv, pair_n, pair_t, pair_c, part, wbuf, gn, kacc, macc,
    ys, yr, xs, xr, ra, rb, xds, xdr, yds, ydr, fin, zf, zs, zr,
    send_sem, recv_sem, in_sem, near, far,
):
    inner, outer = lax.axis_index("inner"), lax.axis_index("outer")
    c, zl = lax.rem(inner, 2), lax.div(inner, 2)
    zh, y, x = lax.rem(outer, 2), lax.rem(lax.div(outer, 2), NY), lax.div(outer, 2 * NY)
    z = zh * NZL + zl

    def at(nx, ny, nz, nc):
        return (lax.rem(nz, NZL) * 2 + nc, (nx * NY + ny) * 2 + lax.div(nz, NZL))

    def x_off(d):
        return lax.rem(x + d + NX, NX)

    def y_off(d):
        return lax.rem(y + d + NY, NY)

    def z_off(d):
        return lax.rem(z + d + NZ, NZ)

    def on_x(d):
        return at(x_off(d), y, z, c)

    def on_y(d):
        return at(x, y_off(d), z, c)

    def on_z(d):
        return at(x, y, z_off(d), c)

    partner = at(x, y, z, 1 - c)
    copies = []

    def send(src, dst, device):
        n = len(copies)
        copy = pltpu.make_async_remote_copy(
            src_ref=src, dst_ref=dst, send_sem=send_sem.at[n], recv_sem=recv_sem.at[n],
            device_id=device, device_id_type=MESH,
        )
        copy.start()
        copies.append(copy)
        return copy

    barrier = pltpu.get_barrier_semaphore()
    for device in (partner, on_z(1), on_z(-1), on_y(1), on_y(-1), on_x(1), on_x(-1)):
        pl.semaphore_signal(barrier, inc=1, device_id=device, device_id_type=MESH)

    loads = []

    def load(src, dst):
        copy = pltpu.make_async_copy(src, dst, in_sem.at[len(loads)])
        copy.start()
        loads.append(copy)
        return copy

    def strip_of(b, core):
        return pl.ds(pl.multiple_of(b * (2 * ROWS) + core * ROWS, ROWS), ROWS)

    load_s = load(scales_h, scales)
    load_w = load(codes_h, codes)
    load_t = [
        load(tok_h.at[:, pl.ds(k * 1024, 1024)], tok.at[:, pl.ds(k * 1024, 1024)]) for k in range(4)
    ]
    load_c = load(cot_h, cot)
    load_n = [load(tok_h.at[:, strip_of(b, c)], pair_n.at[b, pl.ds(0, TOK)]) for b in range(NZL)]

    load_s.wait()
    load_w.wait()
    groups = scales.shape[1]
    row = lax.broadcasted_iota(jnp.int32, (ROWS, groups), 0)
    col = lax.broadcasted_iota(jnp.int32, (ROWS, groups), 1)
    per_row = jnp.where(lax.div(row, ROWS // groups) == col, scales[...], 0.0)
    per_row = jnp.sum(per_row, axis=1, keepdims=True)
    wbuf[0, c] = (codes[...].astype(F32) * per_row).astype(BF16)

    pl.semaphore_wait(barrier, 7)

    n_copies = [
        send(tok_h.at[:, strip_of(b, 1 - c)], pair_n.at[b, pl.ds(TOK, TOK)], partner)
        for b in range(NZL)
    ]

    got = {}

    def slot_of(way, k):
        return k if way > 0 or k in (0, 4) else 4 + k

    def rows_of(h):
        return pl.ds(h * HALF, HALF)

    def pass_on(way, k, h):
        got[way, k + 1, h] = send(
            wbuf.at[slot_of(way, k), c, rows_of(h)],
            wbuf.at[slot_of(way, k + 1), c, rows_of(h)],
            on_z(way),
        )

    def relay(slot, h):
        got["relay", slot, h] = send(
            wbuf.at[slot, c, rows_of(h)], wbuf.at[slot, c, rows_of(h)], partner
        )

    def arrive(way, k, h):
        got[way, k, h].wait_recv()
        if k < 3 or (k == 3 and h == (0 if way > 0 else 1)):
            pass_on(way, k, h)
        relay(slot_of(way, k), h)

    pass_on(1, 0, 0)
    pass_on(-1, 0, 1)
    pass_on(1, 0, 1)
    pass_on(-1, 0, 0)
    relay(0, 0)
    relay(0, 1)
    for d in (1, -1):
        pl.semaphore_signal(near.at[0], inc=1, device_id=on_y(d), device_id_type=MESH)

    total = jnp.zeros((TOK, LANE), F32)
    for k in range(D // LANE):
        if k % 8 == 0:
            load_t[k // 8].wait()
        v = tok[:, k * LANE : (k + 1) * LANE].astype(F32)
        total = total + v * v
    mean = jnp.sum(total, axis=1, keepdims=True) * (1.0 / D)
    inv[...] = jnp.broadcast_to(lax.rsqrt(mean + EPS), (TOK, LANE))
    load_c.wait()
    for k in range(KV // LANE):
        lane = slice(k * LANE, (k + 1) * LANE)
        pair_c[:TOK, lane] = (cot[:, lane].astype(F32) * inv[...]).astype(BF16)
    c_copy = send(pair_c.at[pl.ds(0, TOK)], pair_c.at[pl.ds(TOK, TOK)], partner)

    for b in range(NZL):
        load_n[b].wait()
        n_copies[b].wait_recv()

    def turn(b, _):
        pair_t[b] = pair_n[b].T
        return _

    lax.fori_loop(0, NZL, turn, 0)
    pl.semaphore_wait(near.at[0], 2)
    for d in (2, -2):
        pl.semaphore_signal(near.at[1], inc=1, device_id=on_y(d), device_id_type=MESH)
    c_copy.wait_recv()

    def part_rows(color):
        lane = slice(color * 2 * LANE, (color + 1) * 2 * LANE)

        def rows(b, _):
            p = jnp.dot(pair_t[b], pair_c[:, lane], preferred_element_type=F32)
            part[b, :, :, :, lane] = p.reshape(NX, NY, 8, 2 * LANE)
            return _

        lax.fori_loop(0, NZL, rows, 0)

    def cut(color, q):
        lo = (color * 2 + q % 2) * LANE
        return slice(q // 2 * 4, q // 2 * 4 + 4), slice(lo, lo + LANE)

    def y_part(d, q):
        rows, lane = cut(0, q)
        return part[rows, :, y_off(d), :, lane].reshape(4 * NX * 8, LANE)

    def x_part(d, q):
        rows, lane = cut(1, q)
        return part[rows, x_off(d), :, :, lane].reshape(4 * NY * 8, LANE)

    ring = {}

    def hop(axis, way, q, s):
        n, mine, out, into, on = (
            (NY, y_part, ys, yr, on_y) if axis == "y" else (NX, x_part, xs, xr, on_x)
        )
        last = n // 2
        w = 0 if way > 0 else 1
        first = 1 if q // 2 == w else 2
        v = mine(way * (last + 1 - s), q)
        if s > first:
            ring[axis, way, q, s - 1].wait_recv()
            v = v + into[w, q, s - 2].astype(F32)
        out[w, q, s - 1] = v.astype(BF16)
        ring[axis, way, q, s] = send(out.at[w, q, s - 1], into.at[w, q, s - 1], on(way))

    def hops(axis, s, far_half):
        for k in range(2):
            hop(axis, 1, (0 if far_half else 2) + k, s)
            hop(axis, -1, (2 if far_half else 0) + k, s)

    def ring_sum(axis, q):
        n, mine, into = (NY, y_part, yr) if axis == "y" else (NX, x_part, xr)
        v = mine(0, q)
        for w, way in enumerate((1, -1)):
            ring[axis, way, q, n // 2].wait_recv()
            v = v + into[w, q, n // 2 - 1].astype(F32)
        return v

    def ring_end(axis):
        into, n = (ra, NX) if axis == "y" else (rb, NY)
        for q in (2, 0, 3, 1):
            lo = q % 2 * LANE
            into[q // 2 * 4 : q // 2 * 4 + 4, :, :, lo : lo + LANE] = ring_sum(axis, q).reshape(
                4, n, 8, LANE
            )

    direct = {}

    def x_direct():
        for d in (2, 1, 3):
            xds[d - 1] = ra[:, x_off(d)].reshape(NZL * 8, 2 * LANE).astype(BF16)
            direct["x", d] = send(xds.at[d - 1], xdr.at[d - 1], on_x(d))

    def x_direct_end():
        v = ra[:, x].reshape(NZL * 8, 2 * LANE)
        for d in (1, 3, 2):
            direct["x", d].wait_recv()
            v = v + xdr[d - 1].astype(F32)
        fin[:, :, : 2 * LANE] = v.reshape(NZL, 8, 2 * LANE)

    def y_direct():
        pl.semaphore_wait(near.at[1], 2)
        for d in (4, 3, 5, 2, 6, 1, 7):
            yds[d - 1] = rb[:, y_off(d)].reshape(NZL * 8, 2 * LANE).astype(BF16)
            direct["y", d] = send(yds.at[d - 1], ydr.at[d - 1], on_y(d))

    def y_direct_end():
        v = rb[:, y].reshape(NZL * 8, 2 * LANE)
        for d in range(1, NY):
            direct["y", d].wait_recv()
            v = v + ydr[d - 1].astype(F32)
        fin[:, :, 2 * LANE :] = v.reshape(NZL, 8, 2 * LANE)

    def z_direct():
        for h in range(2):
            v = jnp.concatenate(
                [fin[:, h * 4 : h * 4 + 4, k * LANE : (k + 1) * LANE] for k in range(4)], axis=1
            )
            zf[h] = v
            zs[h] = v.astype(BF16)
        pl.semaphore_wait(far.at[0], 1)
        pl.semaphore_wait(far.at[1], 1)
        for d in range(1, NZ):
            to = z_off(d)
            direct["z", d] = send(
                zs.at[lax.div(to, NZL), lax.rem(to, NZL)], zr.at[d - 1], on_z(d)
            )

    def z_direct_end():
        v = zf[zh, zl]
        for d in range(1, NZ):
            direct["z", d].wait_recv()
            v = v + zr[d - 1].astype(F32)
        for k in range(4):
            grad_weight[:, k * LANE : (k + 1) * LANE] = v[k * 4 : k * 4 + 4]

    kacc[...] = jnp.zeros_like(kacc)
    macc[...] = jnp.zeros_like(macc)

    def chip_of(slot):
        return lax.rem(zl + (NZL - slot if slot < 4 else slot if slot == 4 else slot - 4), NZL)

    def use(slot):
        b = chip_of(slot)
        for h in range(2):
            got["relay", slot, h].wait_recv()
        for p in range(2):
            w = wbuf[slot, p]
            t = tok[:, strip_of(b, p)]
            kacc[...] += jnp.dot(t, w, preferred_element_type=F32)
            g = lax.dot_general(
                cot[...], w, (((1,), (1,)), ((), ())), preferred_element_type=F32
            )
            gn[b, :, p * ROWS : (p + 1) * ROWS] = g
            gx = g * t.astype(F32)
            macc[...] += gx[:, :LANE] + gx[:, LANE:]

    def finish_tokens():
        for k in range(KV // LANE):
            lane = slice(k * LANE, (k + 1) * LANE)
            keys[:, lane] = (kacc[:, lane] * inv[...]).astype(BF16)
        inner_mean = jnp.sum(macc[...] * inv[...], axis=1, keepdims=True) * (1.0 / D)
        macc[...] = jnp.broadcast_to(inner_mean, (TOK, LANE))

        def strip(b, _):
            for q in range(4):
                off = pl.multiple_of(b * (4 * LANE) + q * LANE, LANE)
                nf = tok[:, pl.ds(off, LANE)].astype(F32) * inv[...]
                g = gn[b, :, q * LANE : (q + 1) * LANE]
                grad_tokens[:, pl.ds(off, LANE)] = (inv[...] * (g - nf * macc[...])).astype(BF16)
            return _

        lax.fori_loop(0, NZL, strip, 0)

    def both(k, first):
        arrive(1, k, 0 if first else 1)
        arrive(-1, k, 1 if first else 0)

    def far_signals():
        pl.semaphore_signal(far.at[0], inc=1, device_id=on_z(4), device_id_type=MESH)
        pl.semaphore_signal(far.at[1], inc=1, device_id=on_z(-4), device_id_type=MESH)

    part_rows(0)
    hops("y", 1, True)
    hops("y", 2, False)
    part_rows(1)
    hops("x", 1, True)
    hops("x", 2, False)
    both(1, True)
    hops("y", 2, True)
    both(1, False)
    hops("y", 3, False)
    use(0)
    hops("x", 2, True)
    both(2, True)
    hops("y", 3, True)
    hops("y", 4, False)
    both(2, False)
    use(1)
    hops("y", 4, True)
    both(3, True)
    ring_end("x")
    y_direct()
    ring_end("y")
    x_direct()
    both(3, False)
    use(5)
    use(2)
    both(4, True)
    far_signals()
    x_direct_end()
    use(6)
    y_direct_end()
    z_direct()
    use(3)
    use(7)
    use(4)
    finish_tokens()
    z_direct_end()
    for copy in copies:
        copy.wait_send()


def put_out(keys, grad_tokens, grad_weight, keys_h, grad_tokens_h, grad_weight_h, sem):
    pairs = ((grad_tokens, grad_tokens_h), (keys, keys_h), (grad_weight, grad_weight_h))
    copies = [pltpu.make_async_copy(a, b, sem.at[i]) for i, (a, b) in enumerate(pairs)]
    for copy in copies:
        copy.start()
    for copy in copies:
        copy.wait()


def local(tokens, weight_codes, scales, cotangent):
    vmem = pl.BlockSpec(memory_space=pltpu.VMEM)
    hbm = pl.BlockSpec(memory_space=pl.ANY)
    shapes = (((TOK, KV), BF16), ((TOK, D), BF16), ((4, KV), F32))
    out = pl.pallas_call(
        kernel,
        out_shape=tuple(OUT(*s) for s in shapes),
        in_specs=[pl.BlockSpec(memory_space=pltpu.HBM)] * 4,
        out_specs=(vmem,) * 3,
        scratch_shapes=[
            pltpu.VMEM((TOK, D), BF16),
            pltpu.VMEM((ROWS, KV), BF16),
            pltpu.VMEM((1, ROWS // 4), F32),
            pltpu.VMEM((TOK, KV), BF16),
            pltpu.VMEM((TOK, LANE), F32),
            pltpu.VMEM((NZL, 2 * TOK, ROWS), BF16),
            pltpu.VMEM((NZL, ROWS, 2 * TOK), BF16),
            pltpu.VMEM((2 * TOK, KV), BF16),
            pltpu.VMEM((NZL, NX, NY, 8, KV), F32),
            pltpu.VMEM((8, 2, ROWS, KV), BF16),
            pltpu.VMEM((NZL, TOK, 2 * ROWS), F32),
            pltpu.VMEM((TOK, KV), F32),
            pltpu.VMEM((TOK, LANE), F32),
            pltpu.VMEM((2, 4, NY // 2, 4 * NX * 8, LANE), BF16),
            pltpu.VMEM((2, 4, NY // 2, 4 * NX * 8, LANE), BF16),
            pltpu.VMEM((2, 4, NX // 2, 4 * NY * 8, LANE), BF16),
            pltpu.VMEM((2, 4, NX // 2, 4 * NY * 8, LANE), BF16),
            pltpu.VMEM((NZL, NX, 8, 2 * LANE), F32),
            pltpu.VMEM((NZL, NY, 8, 2 * LANE), F32),
            pltpu.VMEM((NX - 1, NZL * 8, 2 * LANE), BF16),
            pltpu.VMEM((NX - 1, NZL * 8, 2 * LANE), BF16),
            pltpu.VMEM((NY - 1, NZL * 8, 2 * LANE), BF16),
            pltpu.VMEM((NY - 1, NZL * 8, 2 * LANE), BF16),
            pltpu.VMEM((NZL, 8, KV), F32),
            pltpu.VMEM((2, NZL, 16, LANE), F32),
            pltpu.VMEM((2, NZL, 16, LANE), BF16),
            pltpu.VMEM((NZ - 1, 16, LANE), BF16),
            pltpu.SemaphoreType.DMA((N_SEM,)),
            pltpu.SemaphoreType.DMA((N_SEM,)),
            pltpu.SemaphoreType.DMA((16,)),
            pltpu.SemaphoreType.REGULAR((2,)),
            pltpu.SemaphoreType.REGULAR((2,)),
        ],
        compiler_params=pltpu.CompilerParams(
            collective_id=0, has_side_effects=True, vmem_limit_bytes=65_750_000
        ),
        name="key_projection",
    )(tokens, weight_codes, scales.reshape(1, -1), cotangent)
    return pl.pallas_call(
        put_out,
        out_shape=tuple(jax.ShapeDtypeStruct(*s) for s in shapes),
        in_specs=[vmem] * 3,
        out_specs=(hbm,) * 3,
        scratch_shapes=[pltpu.SemaphoreType.DMA((3,))],
        compiler_params=pltpu.CompilerParams(vmem_limit_bytes=16 << 20),
        name="put_out",
    )(*out)


def solution(mesh):
    in_specs = (
        P(("inner", "outer"), None),
        P("inner", None),
        P("inner"),
        P(("inner", "outer"), None),
    )
    out_specs = (P(("inner", "outer"), None),) * 3
    return jax.shard_map(local, mesh=mesh, in_specs=in_specs, out_specs=out_specs, check_vma=False)
```

```python
import jax
import jax.numpy as jnp
from jax import lax
from jax.experimental import pallas as pl
from jax.experimental.pallas import tpu as pltpu
from jax.sharding import PartitionSpec as P

EPS = 1e-05
NX, NY, NZL, NZ = 4, 8, 8, 16
TOK, D, KV = 128, 4096, 512
ROWS = 256
HALF = ROWS // 2
LANE = 128
N_SEM = 136
OUT = pltpu.VMEM
MESH = pl.DeviceIdType.MESH
F32, BF16 = jnp.float32, jnp.bfloat16


def kernel(
    tok_h, codes_h, scales_h, cot_h, keys, grad_tokens, grad_weight,
    tok, codes, scales, cot, inv, cot_n, given, taken, part, wbuf, gn, kacc, macc,
    ys, yr, xs, xr, ra, rb, xds, xdr, yds, ydr, fin, zf, zs, zr,
    send_sem, recv_sem, in_sem, known,
):
    inner, outer = lax.axis_index("inner"), lax.axis_index("outer")
    c, zl = lax.rem(inner, 2), lax.div(inner, 2)
    zh, y, x = lax.rem(outer, 2), lax.rem(lax.div(outer, 2), NY), lax.div(outer, 2 * NY)
    z = zh * NZL + zl

    def at(nx, ny, nz, nc):
        return (lax.rem(nz, NZL) * 2 + nc, (nx * NY + ny) * 2 + lax.div(nz, NZL))

    def x_off(d):
        return lax.rem(x + d + NX, NX)

    def y_off(d):
        return lax.rem(y + d + NY, NY)

    def z_off(d):
        return lax.rem(z + d + NZ, NZ)

    def on_x(d):
        return at(x_off(d), y, z, c)

    def on_y(d):
        return at(x, y_off(d), z, c)

    def on_z(d):
        return at(x, y, z_off(d), c)

    partner = at(x, y, z, 1 - c)
    copies = []

    def send(src, dst, device):
        n = len(copies)
        copy = pltpu.make_async_remote_copy(
            src_ref=src, dst_ref=dst, send_sem=send_sem.at[n], recv_sem=recv_sem.at[n],
            device_id=device, device_id_type=MESH,
        )
        copy.start()
        copies.append(copy)
        return copy

    barrier = pltpu.get_barrier_semaphore()
    for device in (partner, on_z(1), on_z(-1), on_y(1), on_y(-1), on_x(1), on_x(-1)):
        pl.semaphore_signal(barrier, inc=1, device_id=device, device_id_type=MESH)

    loads = []

    def load(src, dst):
        copy = pltpu.make_async_copy(src, dst, in_sem.at[len(loads)])
        copy.start()
        loads.append(copy)
        return copy

    def strip_of(b, core):
        return pl.ds(pl.multiple_of(b * (2 * ROWS) + core * ROWS, ROWS), ROWS)

    load_s = load(scales_h, scales)
    load_w = load(codes_h, codes)
    load_t = [
        load(tok_h.at[:, pl.ds(k * 1024, 1024)], tok.at[:, pl.ds(k * 1024, 1024)]) for k in range(4)
    ]
    load_c = load(cot_h, cot)

    load_s.wait()
    load_w.wait()
    groups = scales.shape[1]
    row = lax.broadcasted_iota(jnp.int32, (ROWS, groups), 0)
    col = lax.broadcasted_iota(jnp.int32, (ROWS, groups), 1)
    per_row = jnp.where(lax.div(row, ROWS // groups) == col, scales[...], 0.0)
    per_row = jnp.sum(per_row, axis=1, keepdims=True)
    wbuf[0, c] = (codes[...].astype(F32) * per_row).astype(BF16)

    total = jnp.zeros((TOK, LANE), F32)
    for k in range(D // LANE):
        if k % 8 == 0:
            load_t[k // 8].wait()
        v = tok[:, k * LANE : (k + 1) * LANE].astype(F32)
        total = total + v * v
    mean = jnp.sum(total, axis=1, keepdims=True) * (1.0 / D)
    inv[...] = jnp.broadcast_to(lax.rsqrt(mean + EPS), (TOK, LANE))
    load_c.wait()
    for k in range(KV // LANE):
        lane = slice(k * LANE, (k + 1) * LANE)
        cot_n[:, lane] = (cot[:, lane].astype(F32) * inv[...]).astype(BF16)
    pl.semaphore_wait(barrier, 7)

    got = {}

    def slot_of(way, k):
        return k if way > 0 or k in (0, 4) else 4 + k

    def rows_of(h):
        return pl.ds(h * HALF, HALF)

    def pass_on(way, k, h):
        got[way, k + 1, h] = send(
            wbuf.at[slot_of(way, k), c, rows_of(h)],
            wbuf.at[slot_of(way, k + 1), c, rows_of(h)],
            on_z(way),
        )

    def relay(slot, h):
        got["relay", slot, h] = send(
            wbuf.at[slot, c, rows_of(h)], wbuf.at[slot, c, rows_of(h)], partner
        )

    def arrive(way, k, h):
        got[way, k, h].wait_recv()
        if k < 3 or (k == 3 and h == (0 if way > 0 else 1)):
            pass_on(way, k, h)
        relay(slot_of(way, k), h)

    pass_on(1, 0, 0)
    pass_on(-1, 0, 1)
    pass_on(1, 0, 1)
    pass_on(-1, 0, 0)
    for d in (1, -1):
        pl.semaphore_signal(known.at[0], inc=1, device_id=on_y(d), device_id_type=MESH)
        pl.semaphore_signal(known.at[0], inc=1, device_id=on_z(d), device_id_type=MESH)

    def rows_for(core, store):
        def rows(b, _):
            store(
                b,
                lax.dot_general(
                    tok[:, strip_of(b, core)], cot_n[...], (((0,), (0,)), ((), ())),
                    preferred_element_type=F32,
                ).reshape(NX, NY, 8, KV),
            )
            return _

        lax.fori_loop(0, NZL, rows, 0, unroll=2)

    def keep(b, v):
        part[b] = v

    def give(b, v):
        given[b] = v.astype(BF16)

    pairs = {}

    def give_block(axis, d):
        if axis == "y":
            at_block = (slice(None), slice(None), y_off(d), slice(None), slice(0, 2 * LANE))
        else:
            at_block = (slice(None), x_off(d), slice(None), slice(None), slice(2 * LANE, KV))
        pairs[axis, d] = send(given.at[at_block], taken.at[at_block], partner)

    def need_block(axis, d):
        copy = pairs.pop((axis, d % (NY if axis == "y" else NX)), None)
        if copy is not None:
            copy.wait_recv()

    rows_for(1 - c, give)
    for axis, d in (
        ("x", 2), ("y", 4), ("x", 1), ("x", 3), ("y", 3), ("y", 5),
        ("y", 2), ("y", 6), ("y", 1), ("y", 7), ("x", 0), ("y", 0),
    ):
        give_block(axis, d)
    relay(0, 0)
    relay(0, 1)
    rows_for(c, keep)

    def cut(color, q):
        lo = (color * 2 + q % 2) * LANE
        return slice(q // 2 * 4, q // 2 * 4 + 4), slice(lo, lo + LANE)

    def y_part(d, q):
        rows, lane = cut(0, q)
        need_block("y", d)
        v = part[rows, :, y_off(d), :, lane] + taken[rows, :, y_off(d), :, lane].astype(F32)
        return v.reshape(4 * NX * 8, LANE)

    def x_part(d, q):
        rows, lane = cut(1, q)
        need_block("x", d)
        v = part[rows, x_off(d), :, :, lane] + taken[rows, x_off(d), :, :, lane].astype(F32)
        return v.reshape(4 * NY * 8, LANE)

    ring = {}

    def hop(axis, way, q, s):
        n, mine, out, into, on = (
            (NY, y_part, ys, yr, on_y) if axis == "y" else (NX, x_part, xs, xr, on_x)
        )
        last = n // 2
        w = 0 if way > 0 else 1
        first = 1 if q // 2 == w else 2
        v = mine(way * (last + 1 - s), q)
        if s > first:
            ring[axis, way, q, s - 1].wait_recv()
            v = v + into[w, q, s - 2].astype(F32)
        out[w, q, s - 1] = v.astype(BF16)
        ring[axis, way, q, s] = send(out.at[w, q, s - 1], into.at[w, q, s - 1], on(way))

    def hops(axis, s, far_half):
        for k in range(2):
            hop(axis, 1, (0 if far_half else 2) + k, s)
            hop(axis, -1, (2 if far_half else 0) + k, s)

    def ring_sum(axis, q):
        n, mine, into = (NY, y_part, yr) if axis == "y" else (NX, x_part, xr)
        v = mine(0, q)
        for w, way in enumerate((1, -1)):
            ring[axis, way, q, n // 2].wait_recv()
            v = v + into[w, q, n // 2 - 1].astype(F32)
        return v

    def ring_end(axis):
        into, n = (ra, NX) if axis == "y" else (rb, NY)
        for q in (2, 0, 3, 1):
            lo = q % 2 * LANE
            into[q // 2 * 4 : q // 2 * 4 + 4, :, :, lo : lo + LANE] = ring_sum(axis, q).reshape(
                4, n, 8, LANE
            )

    direct = {}

    def x_direct():
        for d in (2, 1, 3):
            xds[d - 1] = ra[:, x_off(d)].reshape(NZL * 8, 2 * LANE).astype(BF16)
            direct["x", d] = send(xds.at[d - 1], xdr.at[d - 1], on_x(d))

    def x_direct_end():
        v = ra[:, x].reshape(NZL * 8, 2 * LANE)
        for d in (1, 3, 2):
            direct["x", d].wait_recv()
            v = v + xdr[d - 1].astype(F32)
        fin[:, :, : 2 * LANE] = v.reshape(NZL, 8, 2 * LANE)

    def y_direct():
        for d in (4, 3, 5, 2, 6, 1, 7):
            yds[d - 1] = rb[:, y_off(d)].reshape(NZL * 8, 2 * LANE).astype(BF16)
            direct["y", d] = send(yds.at[d - 1], ydr.at[d - 1], on_y(d))

    def y_direct_end():
        v = rb[:, y].reshape(NZL * 8, 2 * LANE)
        for d in range(1, NY):
            direct["y", d].wait_recv()
            v = v + ydr[d - 1].astype(F32)
        fin[:, :, 2 * LANE :] = v.reshape(NZL, 8, 2 * LANE)

    def z_direct(color):
        lo = color * 2 * LANE
        for h in range(2):
            v = jnp.concatenate(
                [fin[:, h * 4 : h * 4 + 4, lo + k * LANE : lo + (k + 1) * LANE] for k in range(2)],
                axis=1,
            )
            zf[color, h] = v
            zs[color, h] = v.astype(BF16)
        for d in range(1, NZ):
            to = z_off(d)
            direct["z", color, d] = send(
                zs.at[color, lax.div(to, NZL), lax.rem(to, NZL)], zr.at[color, d - 1], on_z(d)
            )

    def z_direct_end(color):
        v = zf[color, zh, zl]
        for d in range(1, NZ):
            direct["z", color, d].wait_recv()
            v = v + zr[color, d - 1].astype(F32)
        for k in range(2):
            lo = (color * 2 + k) * LANE
            grad_weight[:, lo : lo + LANE] = v[k * 4 : k * 4 + 4]

    kacc[...] = jnp.zeros_like(kacc)
    macc[...] = jnp.zeros_like(macc)

    def chip_of(slot):
        return lax.rem(zl + (NZL - slot if slot < 4 else slot if slot == 4 else slot - 4), NZL)

    def use(slot):
        b = chip_of(slot)
        for h in range(2):
            got["relay", slot, h].wait_recv()
        for p in range(2):
            w = wbuf[slot, p]
            t = tok[:, strip_of(b, p)]
            kacc[...] += jnp.dot(t, w, preferred_element_type=F32)
            g = lax.dot_general(
                cot[...], w, (((1,), (1,)), ((), ())), preferred_element_type=F32
            )
            gn[b, :, p * ROWS : (p + 1) * ROWS] = g
            gx = g * t.astype(F32)
            macc[...] += gx[:, :LANE] + gx[:, LANE:]

    def finish_tokens():
        for k in range(KV // LANE):
            lane = slice(k * LANE, (k + 1) * LANE)
            keys[:, lane] = (kacc[:, lane] * inv[...]).astype(BF16)
        inner_mean = jnp.sum(macc[...] * inv[...], axis=1, keepdims=True) * (1.0 / D)
        macc[...] = jnp.broadcast_to(inner_mean, (TOK, LANE))

        def strip(b, _):
            for q in range(4):
                off = pl.multiple_of(b * (4 * LANE) + q * LANE, LANE)
                nf = tok[:, pl.ds(off, LANE)].astype(F32) * inv[...]
                g = gn[b, :, q * LANE : (q + 1) * LANE]
                grad_tokens[:, pl.ds(off, LANE)] = (inv[...] * (g - nf * macc[...])).astype(BF16)
            return _

        lax.fori_loop(0, NZL, strip, 0)

    def both(k, first):
        arrive(1, k, 0 if first else 1)
        arrive(-1, k, 1 if first else 0)

    def know(r):
        pl.semaphore_wait(known.at[r], 4 if r < 2 else 2)
        for d in (2 << r, -2 << r):
            if r == 0:
                pl.semaphore_signal(known.at[1], inc=1, device_id=on_y(d), device_id_type=MESH)
            if r < 2:
                pl.semaphore_signal(known.at[r + 1], inc=1, device_id=on_z(d), device_id_type=MESH)

    hops("x", 1, True)
    hops("x", 2, False)
    hops("y", 1, True)
    hops("y", 2, False)
    know(0)
    both(1, True)
    use(0)
    hops("y", 2, True)
    both(1, False)
    hops("x", 2, True)
    hops("y", 3, False)
    know(1)
    hops("y", 3, True)
    both(2, True)
    hops("y", 4, False)
    use(1)
    both(2, False)
    hops("y", 4, True)
    ring_end("x")
    y_direct()
    use(5)
    use(2)
    both(3, True)
    ring_end("y")
    x_direct()
    know(2)
    use(6)
    x_direct_end()
    z_direct(0)
    both(3, False)
    y_direct_end()
    z_direct(1)
    both(4, True)
    use(3)
    use(7)
    use(4)
    finish_tokens()
    z_direct_end(0)
    z_direct_end(1)
    for copy in copies:
        copy.wait_send()


def put_out(keys, grad_tokens, grad_weight, keys_h, grad_tokens_h, grad_weight_h, sem):
    pairs = ((grad_tokens, grad_tokens_h), (keys, keys_h), (grad_weight, grad_weight_h))
    copies = [pltpu.make_async_copy(a, b, sem.at[i]) for i, (a, b) in enumerate(pairs)]
    for copy in copies:
        copy.start()
    for copy in copies:
        copy.wait()


def local(tokens, weight_codes, scales, cotangent):
    vmem = pl.BlockSpec(memory_space=pltpu.VMEM)
    hbm = pl.BlockSpec(memory_space=pl.ANY)
    shapes = (((TOK, KV), BF16), ((TOK, D), BF16), ((4, KV), F32))
    out = pl.pallas_call(
        kernel,
        out_shape=tuple(OUT(*s) for s in shapes),
        in_specs=[pl.BlockSpec(memory_space=pltpu.HBM)] * 4,
        out_specs=(vmem,) * 3,
        scratch_shapes=[
            pltpu.VMEM((TOK, D), BF16),
            pltpu.VMEM((ROWS, KV), BF16),
            pltpu.VMEM((1, ROWS // 4), F32),
            pltpu.VMEM((TOK, KV), BF16),
            pltpu.VMEM((TOK, LANE), F32),
            pltpu.VMEM((TOK, KV), BF16),
            pltpu.VMEM((NZL, NX, NY, 8, KV), BF16),
            pltpu.VMEM((NZL, NX, NY, 8, KV), BF16),
            pltpu.VMEM((NZL, NX, NY, 8, KV), F32),
            pltpu.VMEM((8, 2, ROWS, KV), BF16),
            pltpu.VMEM((NZL, TOK, 2 * ROWS), F32),
            pltpu.VMEM((TOK, KV), F32),
            pltpu.VMEM((TOK, LANE), F32),
            pltpu.VMEM((2, 4, NY // 2, 4 * NX * 8, LANE), BF16),
            pltpu.VMEM((2, 4, NY // 2, 4 * NX * 8, LANE), BF16),
            pltpu.VMEM((2, 4, NX // 2, 4 * NY * 8, LANE), BF16),
            pltpu.VMEM((2, 4, NX // 2, 4 * NY * 8, LANE), BF16),
            pltpu.VMEM((NZL, NX, 8, 2 * LANE), F32),
            pltpu.VMEM((NZL, NY, 8, 2 * LANE), F32),
            pltpu.VMEM((NX - 1, NZL * 8, 2 * LANE), BF16),
            pltpu.VMEM((NX - 1, NZL * 8, 2 * LANE), BF16),
            pltpu.VMEM((NY - 1, NZL * 8, 2 * LANE), BF16),
            pltpu.VMEM((NY - 1, NZL * 8, 2 * LANE), BF16),
            pltpu.VMEM((NZL, 8, KV), F32),
            pltpu.VMEM((2, 2, NZL, 8, LANE), F32),
            pltpu.VMEM((2, 2, NZL, 8, LANE), BF16),
            pltpu.VMEM((2, NZ - 1, 8, LANE), BF16),
            pltpu.SemaphoreType.DMA((N_SEM,)),
            pltpu.SemaphoreType.DMA((N_SEM,)),
            pltpu.SemaphoreType.DMA((16,)),
            pltpu.SemaphoreType.REGULAR((3,)),
        ],
        compiler_params=pltpu.CompilerParams(
            collective_id=0, has_side_effects=True, vmem_limit_bytes=65_750_000
        ),
        name="key_projection",
    )(tokens, weight_codes, scales.reshape(1, -1), cotangent)
    return pl.pallas_call(
        put_out,
        out_shape=tuple(jax.ShapeDtypeStruct(*s) for s in shapes),
        in_specs=[vmem] * 3,
        out_specs=(hbm,) * 3,
        scratch_shapes=[pltpu.SemaphoreType.DMA((3,))],
        compiler_params=pltpu.CompilerParams(vmem_limit_bytes=16 << 20),
        name="put_out",
    )(*out)


def solution(mesh):
    in_specs = (
        P(("inner", "outer"), None),
        P("inner", None),
        P("inner"),
        P(("inner", "outer"), None),
    )
    out_specs = (P(("inner", "outer"), None),) * 3
    return jax.shard_map(local, mesh=mesh, in_specs=in_specs, out_specs=out_specs, check_vma=False)
```

```python
import jax
import jax.numpy as jnp
from jax import lax
from jax.experimental import pallas as pl
from jax.experimental.pallas import tpu as pltpu
from jax.sharding import PartitionSpec as P

EPS = 1e-05
NX, NY, NZL, NZ = 4, 8, 8, 16
TOK, D, KV = 128, 4096, 512
ROWS = 256
HALF = ROWS // 2
LANE = 128
N_SEM = 136
OUT = pltpu.VMEM
MESH = pl.DeviceIdType.MESH
F32, BF16 = jnp.float32, jnp.bfloat16


def kernel(
    tok_h, codes_h, scales_h, cot_h, keys, grad_tokens, grad_weight,
    tok, codes, scales, cot, inv, cot_n, given, taken, part, wbuf, gn, kacc, macc,
    ys, yr, xs, xr, ra, rb, xds, xdr, yds, ydr, fin, zf, zs, zr,
    send_sem, recv_sem, in_sem, known,
):
    inner, outer = lax.axis_index("inner"), lax.axis_index("outer")
    c, zl = lax.rem(inner, 2), lax.div(inner, 2)
    zh, y, x = lax.rem(outer, 2), lax.rem(lax.div(outer, 2), NY), lax.div(outer, 2 * NY)
    z = zh * NZL + zl

    def at(nx, ny, nz, nc):
        return (lax.rem(nz, NZL) * 2 + nc, (nx * NY + ny) * 2 + lax.div(nz, NZL))

    def x_off(d):
        return lax.rem(x + d + NX, NX)

    def y_off(d):
        return lax.rem(y + d + NY, NY)

    def z_off(d):
        return lax.rem(z + d + NZ, NZ)

    def on_x(d):
        return at(x_off(d), y, z, c)

    def on_y(d):
        return at(x, y_off(d), z, c)

    def on_z(d):
        return at(x, y, z_off(d), c)

    partner = at(x, y, z, 1 - c)
    copies = []

    def send(src, dst, device):
        n = len(copies)
        copy = pltpu.make_async_remote_copy(
            src_ref=src, dst_ref=dst, send_sem=send_sem.at[n], recv_sem=recv_sem.at[n],
            device_id=device, device_id_type=MESH,
        )
        copy.start()
        copies.append(copy)
        return copy

    barrier = pltpu.get_barrier_semaphore()
    for device in (partner, on_z(1), on_z(-1), on_y(1), on_y(-1), on_x(1), on_x(-1)):
        pl.semaphore_signal(barrier, inc=1, device_id=device, device_id_type=MESH)

    loads = []

    def load(src, dst):
        copy = pltpu.make_async_copy(src, dst, in_sem.at[len(loads)])
        copy.start()
        loads.append(copy)
        return copy

    def strip_of(b, core):
        return pl.ds(pl.multiple_of(b * (2 * ROWS) + core * ROWS, ROWS), ROWS)

    load_s = load(scales_h, scales)
    load_w = load(codes_h, codes)
    load_t = [
        load(tok_h.at[:, pl.ds(k * 1024, 1024)], tok.at[:, pl.ds(k * 1024, 1024)]) for k in range(4)
    ]
    load_c = load(cot_h, cot)

    load_s.wait()
    load_w.wait()
    groups = scales.shape[1]
    row = lax.broadcasted_iota(jnp.int32, (ROWS, groups), 0)
    col = lax.broadcasted_iota(jnp.int32, (ROWS, groups), 1)
    per_row = jnp.where(lax.div(row, ROWS // groups) == col, scales[...], 0.0)
    per_row = jnp.sum(per_row, axis=1, keepdims=True)
    wbuf[0, c] = (codes[...].astype(F32) * per_row).astype(BF16)

    total = jnp.zeros((TOK, LANE), F32)
    for k in range(D // LANE):
        if k % 8 == 0:
            load_t[k // 8].wait()
        v = tok[:, k * LANE : (k + 1) * LANE].astype(F32)
        total = total + v * v
    mean = jnp.sum(total, axis=1, keepdims=True) * (1.0 / D)
    inv[...] = jnp.broadcast_to(lax.rsqrt(mean + EPS), (TOK, LANE))
    load_c.wait()
    for k in range(KV // LANE):
        lane = slice(k * LANE, (k + 1) * LANE)
        cot_n[:, lane] = (cot[:, lane].astype(F32) * inv[...]).astype(BF16)
    pl.semaphore_wait(barrier, 7)

    got = {}

    def slot_of(way, k):
        return k if way > 0 or k in (0, 4) else 4 + k

    def rows_of(h):
        return pl.ds(h * HALF, HALF)

    def pass_on(way, k, h):
        got[way, k + 1, h] = send(
            wbuf.at[slot_of(way, k), c, rows_of(h)],
            wbuf.at[slot_of(way, k + 1), c, rows_of(h)],
            on_z(way),
        )

    def relay(slot, h):
        got["relay", slot, h] = send(
            wbuf.at[slot, c, rows_of(h)], wbuf.at[slot, c, rows_of(h)], partner
        )

    def arrive(way, k, h):
        got[way, k, h].wait_recv()
        if k < 3 or (k == 3 and h == (0 if way > 0 else 1)):
            pass_on(way, k, h)
        relay(slot_of(way, k), h)

    pass_on(1, 0, 0)
    pass_on(-1, 0, 1)
    pass_on(1, 0, 1)
    pass_on(-1, 0, 0)
    for d in (1, -1):
        pl.semaphore_signal(known.at[0], inc=1, device_id=on_y(d), device_id_type=MESH)
        pl.semaphore_signal(known.at[0], inc=1, device_id=on_z(d), device_id_type=MESH)

    def rows_for(core, store):
        def rows(b, _):
            store(
                b,
                lax.dot_general(
                    tok[:, strip_of(b, core)], cot_n[...], (((0,), (0,)), ((), ())),
                    preferred_element_type=F32,
                ).reshape(NX, NY, 8, KV),
            )
            return _

        lax.fori_loop(0, NZL, rows, 0, unroll=4)

    def keep(b, v):
        part[b] = v

    def give(b, v):
        given[b] = v.astype(BF16)

    pairs = {}

    def give_block(axis, d):
        if axis == "y":
            at_block = (slice(None), slice(None), y_off(d), slice(None), slice(0, 2 * LANE))
        else:
            at_block = (slice(None), x_off(d), slice(None), slice(None), slice(2 * LANE, KV))
        pairs[axis, d] = send(given.at[at_block], taken.at[at_block], partner)

    def need_block(axis, d):
        copy = pairs.pop((axis, d % (NY if axis == "y" else NX)), None)
        if copy is not None:
            copy.wait_recv()

    rows_for(1 - c, give)
    for axis, d in (
        ("x", 2), ("y", 4), ("x", 1), ("x", 3), ("y", 3), ("y", 5),
        ("y", 2), ("y", 6), ("y", 1), ("y", 7), ("x", 0), ("y", 0),
    ):
        give_block(axis, d)
    relay(0, 0)
    relay(0, 1)
    rows_for(c, keep)

    def cut(color, q):
        lo = (color * 2 + q % 2) * LANE
        return slice(q // 2 * 4, q // 2 * 4 + 4), slice(lo, lo + LANE)

    def y_part(d, q):
        rows, lane = cut(0, q)
        need_block("y", d)
        v = part[rows, :, y_off(d), :, lane] + taken[rows, :, y_off(d), :, lane].astype(F32)
        return v.reshape(4 * NX * 8, LANE)

    def x_part(d, q):
        rows, lane = cut(1, q)
        need_block("x", d)
        v = part[rows, x_off(d), :, :, lane] + taken[rows, x_off(d), :, :, lane].astype(F32)
        return v.reshape(4 * NY * 8, LANE)

    ring = {}

    def hop(axis, way, q, s):
        n, mine, out, into, on = (
            (NY, y_part, ys, yr, on_y) if axis == "y" else (NX, x_part, xs, xr, on_x)
        )
        last = n // 2
        w = 0 if way > 0 else 1
        first = 1 if q // 2 == w else 2
        v = mine(way * (last + 1 - s), q)
        if s > first:
            ring[axis, way, q, s - 1].wait_recv()
            v = v + into[w, q, s - 2].astype(F32)
        out[w, q, s - 1] = v.astype(BF16)
        ring[axis, way, q, s] = send(out.at[w, q, s - 1], into.at[w, q, s - 1], on(way))

    def hops(axis, s, far_half):
        for k in range(2):
            hop(axis, 1, (0 if far_half else 2) + k, s)
            hop(axis, -1, (2 if far_half else 0) + k, s)

    def ring_sum(axis, q):
        n, mine, into = (NY, y_part, yr) if axis == "y" else (NX, x_part, xr)
        v = mine(0, q)
        for w, way in enumerate((1, -1)):
            ring[axis, way, q, n // 2].wait_recv()
            v = v + into[w, q, n // 2 - 1].astype(F32)
        return v

    def ring_end(axis):
        into, n = (ra, NX) if axis == "y" else (rb, NY)
        for q in (2, 0, 3, 1):
            lo = q % 2 * LANE
            into[q // 2 * 4 : q // 2 * 4 + 4, :, :, lo : lo + LANE] = ring_sum(axis, q).reshape(
                4, n, 8, LANE
            )

    direct = {}

    def x_direct():
        for d in (2, 1, 3):
            xds[d - 1] = ra[:, x_off(d)].reshape(NZL * 8, 2 * LANE).astype(BF16)
            direct["x", d] = send(xds.at[d - 1], xdr.at[d - 1], on_x(d))

    def x_direct_end():
        v = ra[:, x].reshape(NZL * 8, 2 * LANE)
        for d in (1, 3, 2):
            direct["x", d].wait_recv()
            v = v + xdr[d - 1].astype(F32)
        fin[:, :, : 2 * LANE] = v.reshape(NZL, 8, 2 * LANE)

    def y_direct():
        for d in (4, 3, 5, 2, 6, 1, 7):
            yds[d - 1] = rb[:, y_off(d)].reshape(NZL * 8, 2 * LANE).astype(BF16)
            direct["y", d] = send(yds.at[d - 1], ydr.at[d - 1], on_y(d))

    def y_direct_end():
        v = rb[:, y].reshape(NZL * 8, 2 * LANE)
        for d in range(1, NY):
            direct["y", d].wait_recv()
            v = v + ydr[d - 1].astype(F32)
        fin[:, :, 2 * LANE :] = v.reshape(NZL, 8, 2 * LANE)

    def z_direct(color):
        lo = color * 2 * LANE
        for h in range(2):
            v = jnp.concatenate(
                [fin[:, h * 4 : h * 4 + 4, lo + k * LANE : lo + (k + 1) * LANE] for k in range(2)],
                axis=1,
            )
            zf[color, h] = v
            zs[color, h] = v.astype(BF16)
        for d in range(1, NZ):
            to = z_off(d)
            direct["z", color, d] = send(
                zs.at[color, lax.div(to, NZL), lax.rem(to, NZL)], zr.at[color, d - 1], on_z(d)
            )

    def z_direct_end(color):
        v = zf[color, zh, zl]
        for d in range(1, NZ):
            direct["z", color, d].wait_recv()
            v = v + zr[color, d - 1].astype(F32)
        for k in range(2):
            lo = (color * 2 + k) * LANE
            grad_weight[:, lo : lo + LANE] = v[k * 4 : k * 4 + 4]

    kacc[...] = jnp.zeros_like(kacc)
    macc[...] = jnp.zeros_like(macc)

    def chip_of(slot):
        return lax.rem(zl + (NZL - slot if slot < 4 else slot if slot == 4 else slot - 4), NZL)

    def use(slot):
        b = chip_of(slot)
        for h in range(2):
            got["relay", slot, h].wait_recv()
        for p in range(2):
            w = wbuf[slot, p]
            t = tok[:, strip_of(b, p)]
            kacc[...] += jnp.dot(t, w, preferred_element_type=F32)
            g = lax.dot_general(
                cot[...], w, (((1,), (1,)), ((), ())), preferred_element_type=F32
            )
            gn[b, :, p * ROWS : (p + 1) * ROWS] = g
            gx = g * t.astype(F32)
            macc[...] += gx[:, :LANE] + gx[:, LANE:]

    def finish_tokens():
        for k in range(KV // LANE):
            lane = slice(k * LANE, (k + 1) * LANE)
            keys[:, lane] = (kacc[:, lane] * inv[...]).astype(BF16)
        inner_mean = jnp.sum(macc[...] * inv[...], axis=1, keepdims=True) * (1.0 / D)
        macc[...] = jnp.broadcast_to(inner_mean, (TOK, LANE))

        def strip(b, _):
            for q in range(4):
                off = pl.multiple_of(b * (4 * LANE) + q * LANE, LANE)
                nf = tok[:, pl.ds(off, LANE)].astype(F32) * inv[...]
                g = gn[b, :, q * LANE : (q + 1) * LANE]
                grad_tokens[:, pl.ds(off, LANE)] = (inv[...] * (g - nf * macc[...])).astype(BF16)
            return _

        lax.fori_loop(0, NZL, strip, 0)

    def both(k, first):
        arrive(1, k, 0 if first else 1)
        arrive(-1, k, 1 if first else 0)

    def know(r):
        pl.semaphore_wait(known.at[r], 4 if r < 2 else 2)
        for d in (2 << r, -2 << r):
            if r == 0:
                pl.semaphore_signal(known.at[1], inc=1, device_id=on_y(d), device_id_type=MESH)
            if r < 2:
                pl.semaphore_signal(known.at[r + 1], inc=1, device_id=on_z(d), device_id_type=MESH)

    hops("x", 1, True)
    hops("x", 2, False)
    hops("y", 1, True)
    hops("y", 2, False)
    know(0)
    both(1, True)
    use(0)
    hops("y", 2, True)
    hops("x", 2, True)
    hops("y", 3, False)
    both(1, False)
    know(1)
    hops("y", 3, True)
    use(1)
    hops("y", 4, False)
    both(2, True)
    hops("y", 4, True)
    ring_end("x")
    y_direct()
    both(2, False)
    use(5)
    ring_end("y")
    x_direct()
    both(3, True)
    know(2)
    use(2)
    use(6)
    x_direct_end()
    z_direct(0)
    both(3, False)
    y_direct_end()
    z_direct(1)
    both(4, True)
    use(3)
    use(7)
    use(4)
    finish_tokens()
    for copy in copies:
        copy.wait_send()
    z_direct_end(0)
    z_direct_end(1)


def put_out(keys, grad_tokens, grad_weight, keys_h, grad_tokens_h, grad_weight_h, sem):
    pairs = ((grad_tokens, grad_tokens_h), (keys, keys_h), (grad_weight, grad_weight_h))
    copies = [pltpu.make_async_copy(a, b, sem.at[i]) for i, (a, b) in enumerate(pairs)]
    for copy in copies:
        copy.start()
    for copy in copies:
        copy.wait()


def local(tokens, weight_codes, scales, cotangent):
    vmem = pl.BlockSpec(memory_space=pltpu.VMEM)
    hbm = pl.BlockSpec(memory_space=pl.ANY)
    shapes = (((TOK, KV), BF16), ((TOK, D), BF16), ((4, KV), F32))
    out = pl.pallas_call(
        kernel,
        out_shape=tuple(OUT(*s) for s in shapes),
        in_specs=[pl.BlockSpec(memory_space=pltpu.HBM)] * 4,
        out_specs=(vmem,) * 3,
        scratch_shapes=[
            pltpu.VMEM((TOK, D), BF16),
            pltpu.VMEM((ROWS, KV), BF16),
            pltpu.VMEM((1, ROWS // 4), F32),
            pltpu.VMEM((TOK, KV), BF16),
            pltpu.VMEM((TOK, LANE), F32),
            pltpu.VMEM((TOK, KV), BF16),
            pltpu.VMEM((NZL, NX, NY, 8, KV), BF16),
            pltpu.VMEM((NZL, NX, NY, 8, KV), BF16),
            pltpu.VMEM((NZL, NX, NY, 8, KV), F32),
            pltpu.VMEM((8, 2, ROWS, KV), BF16),
            pltpu.VMEM((NZL, TOK, 2 * ROWS), F32),
            pltpu.VMEM((TOK, KV), F32),
            pltpu.VMEM((TOK, LANE), F32),
            pltpu.VMEM((2, 4, NY // 2, 4 * NX * 8, LANE), BF16),
            pltpu.VMEM((2, 4, NY // 2, 4 * NX * 8, LANE), BF16),
            pltpu.VMEM((2, 4, NX // 2, 4 * NY * 8, LANE), BF16),
            pltpu.VMEM((2, 4, NX // 2, 4 * NY * 8, LANE), BF16),
            pltpu.VMEM((NZL, NX, 8, 2 * LANE), F32),
            pltpu.VMEM((NZL, NY, 8, 2 * LANE), F32),
            pltpu.VMEM((NX - 1, NZL * 8, 2 * LANE), BF16),
            pltpu.VMEM((NX - 1, NZL * 8, 2 * LANE), BF16),
            pltpu.VMEM((NY - 1, NZL * 8, 2 * LANE), BF16),
            pltpu.VMEM((NY - 1, NZL * 8, 2 * LANE), BF16),
            pltpu.VMEM((NZL, 8, KV), F32),
            pltpu.VMEM((2, 2, NZL, 8, LANE), F32),
            pltpu.VMEM((2, 2, NZL, 8, LANE), BF16),
            pltpu.VMEM((2, NZ - 1, 8, LANE), BF16),
            pltpu.SemaphoreType.DMA((N_SEM,)),
            pltpu.SemaphoreType.DMA((N_SEM,)),
            pltpu.SemaphoreType.DMA((16,)),
            pltpu.SemaphoreType.REGULAR((3,)),
        ],
        compiler_params=pltpu.CompilerParams(
            collective_id=0, has_side_effects=True, vmem_limit_bytes=65_750_000
        ),
        name="key_projection",
    )(tokens, weight_codes, scales.reshape(1, -1), cotangent)
    return pl.pallas_call(
        put_out,
        out_shape=tuple(jax.ShapeDtypeStruct(*s) for s in shapes),
        in_specs=[vmem] * 3,
        out_specs=(hbm,) * 3,
        scratch_shapes=[pltpu.SemaphoreType.DMA((3,))],
        compiler_params=pltpu.CompilerParams(vmem_limit_bytes=16 << 20),
        name="put_out",
    )(*out)


def solution(mesh):
    in_specs = (
        P(("inner", "outer"), None),
        P("inner", None),
        P("inner"),
        P(("inner", "outer"), None),
    )
    out_specs = (P(("inner", "outer"), None),) * 3
    return jax.shard_map(local, mesh=mesh, in_specs=in_specs, out_specs=out_specs, check_vma=False)
```
